128 devices in a mesh: chan: 16 (over z, y_hi, core), win: 8 (over x, y_lo).
Axes of the slice: x: 4, y: 4 (y_hi: 2, y_lo: 2; y = y_hi * 2 + y_lo), z: 4, core: 2. Of those that a mesh axis runs over, the one named last changes fastest.
Arguments:
- waves: float32 [1024, 16384], P('chan', 'win'), may hold values from -40 to 40
- matchings: int32 [3, 16], replicated, may hold values from 0 to 15, as said below
- lag_offset: int32 [3, 16], replicated, may hold values from -64 to 64
Outputs:
- stacked: float32 [64, 3, 1024, 256], P('win', None, 'chan')
The draws below stay inside these ranges and needn't reach their ends.
Inputs may be any that keep to these rules, and one draw needn't show every extreme that they name: `matchings`: each row pairs the 16 blocks two by two: the partner of a block's partner is the block itself, and no block is its own partner.
All inputs are finite; a program needn't handle non-finite values.
Results may differ from the reference program's by a relative error of at most 0.012.
Values may be sent and summed in bfloat16 or wider, within the bound.
No kernel may reach another device: no remote copies, remote signals or barrier semaphores. Data moves between devices by JAX's collectives and lax.ppermute only.
A program may use at most 128 MiB of HBM per device.

```python
import math
import jax
import jax.numpy as jnp
from jax import lax

CHAN_BLOCK = 64
WIN_LEN = 2048
LAG_COUNT = 256
MATCHINGS = 3
OFFSET_MOST = 64
BLOCKS = 16
WINDOWS = 8
CHANNELS = 1024
SAMPLES = 16384


def draw_waves(key, part):
    noise_key, scale_key = jax.random.split(key)
    piece_len = 64
    noise = jax.random.truncated_normal(noise_key, -4.0, 4.0, (CHANNELS, SAMPLES), jnp.float32)
    levels = jnp.exp(jax.random.uniform(scale_key, (CHANNELS, SAMPLES // piece_len), jnp.float32, 0.0, math.log(10.0)))
    return noise * jnp.repeat(levels, piece_len, axis=1)


def draw_matchings(key, part):
    pairings = []
    for matching_index in range(MATCHINGS):
        shuffled = jax.random.permutation(jax.random.fold_in(key, matching_index), BLOCKS).astype(jnp.int32)
        swapped = shuffled.reshape(BLOCKS // 2, 2)[:, ::-1].reshape(BLOCKS)
        pairings.append(jnp.zeros((BLOCKS,), jnp.int32).at[shuffled].set(swapped))
    return jnp.stack(pairings)


def draw_lag_offset(key, part):
    base_key, first_key, second_key = jax.random.split(key, 3)
    entries = MATCHINGS * BLOCKS
    values = jax.random.randint(base_key, (entries,), -OFFSET_MOST, OFFSET_MOST + 1).astype(jnp.int32)
    first_pick = jax.random.randint(first_key, (), 0, entries)
    second_pick = (first_pick + 1 + jax.random.randint(second_key, (), 0, entries - 1)) % entries
    positions = jnp.arange(entries, dtype=jnp.int32)
    values = jnp.where(positions == first_pick, OFFSET_MOST, jnp.where(positions == second_pick, -OFFSET_MOST, values))
    return values.astype(jnp.int32).reshape(MATCHINGS, BLOCKS)


def setup_inputs(seed: int = 0) -> dict:
    splits = jax.random.split(jax.random.key(seed), 4)
    return {
        "waves": draw_waves(jax.random.fold_in(splits[3], 71), 0),
        "matchings": draw_matchings(jax.random.fold_in(splits[3], 71), 0),
        "lag_offset": draw_lag_offset(jax.random.fold_in(splits[3], 71), 0),
    }


def whiten(waves):
    traces = waves.reshape(CHANNELS, WINDOWS, WIN_LEN)
    power_mean = lax.optimization_barrier(jnp.mean(traces * traces, axis=2, keepdims=True))
    return (traces / jnp.sqrt(power_mean + 1e-06)).astype(jnp.bfloat16)

def reference(waves, matchings, lag_offset):
    whitened = whiten(waves).astype(jnp.float32).reshape(BLOCKS, CHAN_BLOCK, WINDOWS, WIN_LEN)
    margin = LAG_COUNT // 2 + OFFSET_MOST
    padded = jnp.pad(whitened, ((0, 0), (0, 0), (0, 0), (margin, margin)))
    factor = 1.0 / math.sqrt(WIN_LEN * WINDOWS)
    lag_steps = jnp.arange(LAG_COUNT, dtype=jnp.int32)

    def one_pair(flat_index):
        matching_index = flat_index // BLOCKS
        block_index = flat_index % BLOCKS
        partner = matchings[matching_index, block_index]
        offset = lag_offset[matching_index, block_index]
        starts = (margin + offset - LAG_COUNT // 2 + lag_steps).astype(jnp.int32)

        def one_window(window_index, running):
            source = whitened[block_index, :, window_index, :]
            target = padded[partner, :, window_index, :]
            shifted = jax.vmap(lambda first_index: lax.dynamic_slice_in_dim(target, first_index, WIN_LEN, 1))(starts)
            products = jnp.einsum('at,jbt->baj', source, shifted, precision=lax.Precision.HIGHEST)
            return running + (products * factor).astype(jnp.bfloat16).astype(jnp.float32)
        return lax.fori_loop(0, WINDOWS, one_window, jnp.zeros((CHAN_BLOCK, CHAN_BLOCK, LAG_COUNT), jnp.float32))
    stacks = lax.map(one_pair, jnp.arange(MATCHINGS * BLOCKS, dtype=jnp.int32))
    stacks = stacks.reshape(MATCHINGS, BLOCKS, CHAN_BLOCK, CHAN_BLOCK, LAG_COUNT)
    return jnp.transpose(stacks, (2, 0, 1, 3, 4)).reshape(CHAN_BLOCK, MATCHINGS, CHANNELS, LAG_COUNT)
```

```python
import jax
import jax.numpy as jnp
from jax import lax
from jax.experimental import pallas as pl
from jax.experimental.pallas import tpu as pltpu
from jax.sharding import PartitionSpec as P

CHANS = 64
LEN = 2048
BLOCKS = 16
WINS = 8
MATCH = 3
LAGS = 256
ROWS = CHANS // WINS
GROUPS = 8
FINE = LAGS // GROUPS
DEPTH = LEN + LAGS
WIDE = LEN + 512
HALF = LEN // 2
SCALE = 1.0 / 128.0


def whiten_kernel(x_ref, cut_ref, turned_ref):
    x = x_ref[...]
    power = jnp.mean(x * x, axis=1, keepdims=True)
    white = x / jnp.sqrt(power + 1e-06)
    for c in range(BLOCKS):
        for g in range(WINS):
            cut_ref[c, g] = white[g * ROWS:(g + 1) * ROWS, 128 * c:128 * (c + 1)].astype(jnp.bfloat16)
    halves = jnp.concatenate([white[:, :HALF], white[:, HALF:]], axis=0)
    turned = halves.T.astype(jnp.bfloat16)
    for w in range(WINS):
        turned_ref[w] = turned


def whiten(x):
    return pl.pallas_call(
        whiten_kernel,
        out_shape=(
            jax.ShapeDtypeStruct((BLOCKS, WINS, ROWS, 128), jnp.bfloat16),
            jax.ShapeDtypeStruct((WINS, HALF, 128), jnp.bfloat16),
        ),
        name="whiten",
    )(x)


def choose_kernel(match_ref, from_ref, to_ref):
    for d in range(BLOCKS):
        for m in range(MATCH):
            to_ref[d, m] = from_ref[match_ref[m, d]]


def choose(matchings, chunks):
    return pl.pallas_call(
        choose_kernel,
        out_shape=jax.ShapeDtypeStruct((BLOCKS, MATCH, WINS, ROWS, 128), jnp.bfloat16),
        in_specs=[pl.BlockSpec(memory_space=pltpu.SMEM), pl.BlockSpec(memory_space=pltpu.VMEM)],
        name="choose",
    )(matchings, chunks)


def corr_kernel(offs, s_ref, t_ref, o_ref, sd, ts, acc):
    w = pl.program_id(0)
    m = pl.program_id(1)

    @pl.when((w == 0) & (m == 0))
    def _():
        sd[...] = jnp.zeros_like(sd)

    @pl.when(m == 0)
    def _():
        for h in range(2):
            piece = s_ref[0, :, h * CHANS:(h + 1) * CHANS]
            for jl in range(GROUPS):
                first = FINE * jl + HALF * h
                sd[first:first + HALF, jl * CHANS:(jl + 1) * CHANS] = piece

    zeros = jnp.zeros((ROWS, 256), jnp.float32)
    row = jnp.concatenate([zeros] + [t_ref[c, 0, 0].astype(jnp.float32) for c in range(BLOCKS)] + [zeros], axis=1)
    even = pltpu.roll(row, WIDE - 128 - offs[m], 1)
    odd = pltpu.roll(even, WIDE - 1, 1)
    both = jnp.concatenate([even, odd], axis=0).astype(jnp.bfloat16)
    for k in range(FINE // 2):
        ts[16 * k:16 * k + 16, :] = both[:, 2 * k:2 * k + DEPTH]
    r = jnp.dot(ts[...], sd[...], preferred_element_type=jnp.float32)
    for q in range(GROUPS // 2):
        part = r[:, 128 * q:128 * (q + 1)]

        @pl.when(w == 0)
        def _():
            acc[m, q] = part

        @pl.when(w > 0)
        def _():
            acc[m, q] = acc[m, q] + part

    @pl.when(w == WINS - 1)
    def _():
        for b in range(ROWS):
            lags = [acc[m, q, pl.ds(b, FINE, stride=ROWS), :] * SCALE for q in range(GROUPS // 2)]
            turned = jnp.concatenate(
                [lags[jl // 2][:, (jl % 2) * CHANS:(jl % 2 + 1) * CHANS] for jl in range(GROUPS)], axis=0
            )
            o_ref[b, m] = turned.T


def corr(offs, source, partner):
    return pl.pallas_call(
        corr_kernel,
        out_shape=jax.ShapeDtypeStruct((ROWS, MATCH, CHANS, LAGS), jnp.float32),
        grid_spec=pltpu.PrefetchScalarGridSpec(
            num_scalar_prefetch=1,
            grid=(WINS, MATCH),
            in_specs=[
                pl.BlockSpec((1, HALF, 128), lambda w, m, o: (w, 0, 0)),
                pl.BlockSpec((BLOCKS, 1, 1, ROWS, 128), lambda w, m, o: (0, m, w, 0, 0)),
            ],
            out_specs=pl.BlockSpec((ROWS, MATCH, CHANS, LAGS), lambda w, m, o: (0, 0, 0, 0)),
            scratch_shapes=[
                pltpu.VMEM((DEPTH, GROUPS * CHANS), jnp.bfloat16),
                pltpu.VMEM((FINE * ROWS, DEPTH), jnp.bfloat16),
                pltpu.VMEM((MATCH, GROUPS // 2, FINE * ROWS, 128), jnp.float32),
            ],
        ),
        name="corr",
    )(offs, source, partner)


def local(waves, matchings, lag_offset):
    offs = lax.dynamic_index_in_dim(lag_offset, lax.axis_index("chan"), 1, keepdims=False)
    cut, turned = whiten(waves)
    chunks = lax.all_to_all(cut.reshape(BLOCKS * WINS, ROWS, 128), ("chan", "win"), 0, 0)
    source = lax.all_to_all(turned, "win", 0, 0)
    sent = choose(matchings, chunks.reshape(BLOCKS, WINS, ROWS, 128))
    partner = lax.all_to_all(sent, "chan", 0, 0)
    return corr(offs, source, partner)


def solution(mesh):
    return jax.shard_map(
        local,
        mesh=mesh,
        in_specs=(P("chan", "win"), P(), P()),
        out_specs=P("win", None, "chan", None),
        check_vma=False,
    )
```

```python
import jax
import jax.numpy as jnp
from jax import lax
from jax.experimental import pallas as pl
from jax.experimental.pallas import tpu as pltpu
from jax.sharding import PartitionSpec as P

CHANS = 64
LEN = 2048
HALF = LEN // 2
BLOCKS = 16
WINS = 8
MATCH = 3
LAGS = 256
ROWS = CHANS // WINS
FINE = 16
GROUPS = 128 // FINE
SPAN = LEN + 128
WIDE = LEN + 512
PAD = 96
PAIR = 2
SCALE = 1.0 / 128.0


def whiten_kernel(x_ref, cut_ref, turned_ref):
    x = x_ref[...]
    power = jnp.mean(x * x, axis=1, keepdims=True)
    white = x / jnp.sqrt(power + 1e-06)
    for c in range(BLOCKS):
        for g in range(WINS):
            cut_ref[c, g] = white[g * ROWS:(g + 1) * ROWS, 128 * c:128 * (c + 1)].astype(jnp.bfloat16)
    halves = jnp.concatenate([white[:, :HALF], white[:, HALF:]], axis=0)
    turned_ref[...] = halves.T.astype(jnp.bfloat16)


def whiten(x):
    return pl.pallas_call(
        whiten_kernel,
        out_shape=(
            jax.ShapeDtypeStruct((BLOCKS, WINS, ROWS, 128), jnp.bfloat16),
            jax.ShapeDtypeStruct((HALF, 128), jnp.bfloat16),
        ),
        compiler_params=pltpu.CompilerParams(vmem_limit_bytes=4 << 20),
        name="whiten",
    )(x)


def choose_kernel(match_ref, from_ref, to_ref):
    for d in range(BLOCKS):
        for m in range(MATCH):
            to_ref[d, m] = from_ref[match_ref[m, d]]


def choose(matchings, chunks):
    return pl.pallas_call(
        choose_kernel,
        out_shape=jax.ShapeDtypeStruct((BLOCKS, MATCH, WINS, ROWS, 128), jnp.bfloat16),
        in_specs=[pl.BlockSpec(memory_space=pltpu.SMEM), pl.BlockSpec(memory_space=pltpu.VMEM)],
        compiler_params=pltpu.CompilerParams(vmem_limit_bytes=4 << 20),
        name="choose",
    )(matchings, chunks)


def corr_kernel(offs, s0_ref, s1_ref, s2_ref, s3_ref, t_ref, o_ref, y0, y1, ts0, ts1, acc):
    lane = lax.broadcasted_iota(jnp.int32, (1, 128), 1)
    mine = offs[MATCH]
    sources = (s0_ref, s1_ref, s2_ref, s3_ref)

    def source(r, y):
        for n in range(PAIR):
            x = sources[r][n].astype(jnp.float32)
            swapped = pltpu.roll(x, CHANS, 1)
            gap = jnp.zeros((FINE, 128), jnp.float32)
            now = jnp.concatenate([x, swapped, gap], axis=0)
            late = jnp.concatenate([gap, swapped, x], axis=0)
            y[n, PAD:PAD + LEN + FINE, :] = jnp.where(lane < CHANS, now, late).astype(jnp.bfloat16)

    def partner(r, ts):
        zeros = jnp.zeros((ROWS, 256), jnp.float32)
        for n in range(PAIR):
            w = lax.bitwise_xor(mine, 2 * r + n)
            for m in range(MATCH):
                cut = [t_ref[c, m, w].astype(jnp.float32) for c in range(BLOCKS)]
                row = jnp.concatenate([zeros] + cut + [zeros], axis=1)
                even = pltpu.roll(row, WIDE - 128 - offs[m], 1)
                odd = pltpu.roll(even, WIDE - 1, 1)
                both = jnp.concatenate([even, odd], axis=0).astype(jnp.bfloat16)
                for k in range(FINE // 2):
                    first = 128 * m + 16 * k
                    ts[n, first:first + 16, :] = both[:, 2 * k:2 * k + SPAN + 128]

    def product(y, ts, fresh):
        lhs = jnp.concatenate(
            [
                jnp.concatenate([ts[n, :, 128 * top:128 * top + SPAN] for n in range(PAIR)], axis=1)
                for top in range(2)
            ],
            axis=0,
        )
        rhs = jnp.concatenate(
            [
                jnp.concatenate([y[n, PAD - 2 * FINE * q:PAD - 2 * FINE * q + SPAN, :] for n in range(PAIR)], axis=0)
                for q in range(GROUPS // 2)
            ],
            axis=1,
        )
        r = jnp.dot(lhs, rhs, preferred_element_type=jnp.float32)
        for q in range(GROUPS // 2):
            part = r[:, 128 * q:128 * (q + 1)]
            acc[q] = part if fresh else acc[q] + part

    for y in (y0, y1):
        for n in range(PAIR):
            y[n, :PAD, :] = jnp.zeros((PAD, 128), jnp.bfloat16)
            y[n, PAD + LEN + FINE:, :] = jnp.zeros((SPAN - LEN - FINE, 128), jnp.bfloat16)
    buffers = ((y0, ts0), (y1, ts1))
    rounds = WINS // PAIR
    source(0, y0)
    partner(0, ts0)
    for r in range(rounds):
        if r + 1 < rounds:
            source(r + 1, buffers[(r + 1) % 2][0])
            partner(r + 1, buffers[(r + 1) % 2][1])
        product(*buffers[r % 2], r == 0)

    for top in range(2):
        for m in range(MATCH):
            for b in range(0, ROWS, 2):
                base = (top * MATCH + m) * 128 + b
                rows = []
                for q in range(GROUPS // 2):
                    lo = acc[q, pl.ds(base, FINE, stride=ROWS), :] * SCALE
                    hi = acc[q, pl.ds(base + 1, FINE, stride=ROWS), :] * SCALE
                    rows.append(jnp.where(lane < CHANS, lo, pltpu.roll(hi, CHANS, 1)))
                    rows.append(jnp.where(lane < CHANS, pltpu.roll(lo, CHANS, 1), hi))
                z = jnp.concatenate(rows, axis=0).T
                o_ref[b, m, :, 128 * top:128 * (top + 1)] = z[:CHANS]
                o_ref[b + 1, m, :, 128 * top:128 * (top + 1)] = z[CHANS:]


def corr(offs, sources, partner):
    vmem = pl.BlockSpec(memory_space=pltpu.VMEM)
    return pl.pallas_call(
        corr_kernel,
        out_shape=jax.ShapeDtypeStruct((ROWS, MATCH, CHANS, LAGS), jnp.float32),
        in_specs=[pl.BlockSpec(memory_space=pltpu.SMEM)] + [vmem] * 5,
        out_specs=vmem,
        scratch_shapes=[pltpu.VMEM((PAIR, PAD + SPAN, 128), jnp.bfloat16)] * 2
        + [pltpu.VMEM((PAIR, MATCH * FINE * ROWS, SPAN + 128), jnp.bfloat16)] * 2
        + [pltpu.VMEM((GROUPS // 2, 2 * MATCH * FINE * ROWS, 128), jnp.float32)],
        compiler_params=pltpu.CompilerParams(vmem_limit_bytes=28 << 20),
        name="corr",
    )(offs, *sources, partner)


def local(waves, matchings, lag_offset):
    win = lax.axis_index("win")
    offs = lax.dynamic_index_in_dim(lag_offset, lax.axis_index("chan"), 1, keepdims=False)
    offs = jnp.concatenate([offs, jnp.full((1,), win, jnp.int32)])
    cut, turned = whiten(waves)
    chunks = lax.all_to_all(cut.reshape(BLOCKS * WINS, ROWS, 128), ("chan", "win"), 0, 0)
    other = lax.ppermute(turned, "win", [(i, i ^ 1) for i in range(WINS)])
    pair = jnp.stack([turned, other])
    far = []
    for r in (1, 2, 3):
        far.append(lax.ppermute(pair, "win", [(i, i ^ (2 * r)) for i in range(WINS)]))
    sent = choose(matchings, chunks.reshape(BLOCKS, WINS, ROWS, 128))
    partner = lax.all_to_all(sent, "chan", 0, 0)
    return corr(offs, [pair] + far, partner)


def solution(mesh):
    return jax.shard_map(
        local,
        mesh=mesh,
        in_specs=(P("chan", "win"), P(), P()),
        out_specs=P("win", None, "chan", None),
        check_vma=False,
    )
```

```python
import jax
import jax.numpy as jnp
from jax import lax
from jax.experimental import pallas as pl
from jax.experimental.pallas import tpu as pltpu
from jax.sharding import PartitionSpec as P

CHANS = 64
LEN = 2048
HALF = LEN // 2
BLOCKS = 16
WINS = 8
MATCH = 3
LAGS = 256
ROWS = CHANS // WINS
FINE = 16
GROUPS = 128 // FINE
SPAN = LEN + 128
WIDE = LEN + 512
PAD = 96
PAIR = 2
NEAR = (SPAN // 128 + 1) // 2
SCALE = 1.0 / 128.0


def whiten_kernel(x_ref, cut_ref, turned_ref):
    x = x_ref[...]
    power = jnp.mean(x * x, axis=1, keepdims=True)
    white = x / jnp.sqrt(power + 1e-06)
    for c in range(BLOCKS):
        for g in range(WINS):
            cut_ref[c, g] = white[g * ROWS:(g + 1) * ROWS, 128 * c:128 * (c + 1)].astype(jnp.bfloat16)
    halves = jnp.concatenate([white[:, :HALF], white[:, HALF:]], axis=0)
    turned_ref[...] = halves.T.astype(jnp.bfloat16)


def whiten(x):
    return pl.pallas_call(
        whiten_kernel,
        out_shape=(
            jax.ShapeDtypeStruct((BLOCKS, WINS, ROWS, 128), jnp.bfloat16),
            jax.ShapeDtypeStruct((HALF, 128), jnp.bfloat16),
        ),
        compiler_params=pltpu.CompilerParams(vmem_limit_bytes=4 << 20),
        name="whiten",
    )(x)


def choose_kernel(match_ref, from_ref, to_ref):
    for d in range(BLOCKS):
        for m in range(MATCH):
            to_ref[d, m] = from_ref[match_ref[m, d]]


def choose(matchings, chunks):
    return pl.pallas_call(
        choose_kernel,
        out_shape=jax.ShapeDtypeStruct((BLOCKS, MATCH, WINS, ROWS, 128), jnp.bfloat16),
        in_specs=[pl.BlockSpec(memory_space=pltpu.SMEM), pl.BlockSpec(memory_space=pltpu.VMEM)],
        compiler_params=pltpu.CompilerParams(vmem_limit_bytes=4 << 20),
        name="choose",
    )(matchings, chunks)


def corr_kernel(offs, s0_ref, s1_ref, s2_ref, s3_ref, t_ref, o_ref, y0, y1, v0, v1, e0, e1, d0, d1, t0, t1, acc):
    lane = lax.broadcasted_iota(jnp.int32, (1, 128), 1)
    mine = offs[MATCH]
    sources = (s0_ref, s1_ref, s2_ref, s3_ref)

    def source(r, y, v):
        for n in range(PAIR):
            x = sources[r][n].astype(jnp.float32)
            swapped = pltpu.roll(x, CHANS, 1)
            gap = jnp.zeros((FINE, 128), jnp.float32)
            now = jnp.concatenate([x, swapped, gap], axis=0)
            late = jnp.concatenate([gap, swapped, x], axis=0)
            both = jnp.where(lane < CHANS, now, late)
            y[n, PAD:PAD + LEN + FINE, :] = both.astype(jnp.bfloat16)
            v[n, PAD:PAD + LEN + FINE - 128, :] = (both[:-128] + both[128:]).astype(jnp.bfloat16)
            v[n, :PAD, :] = both[128 - PAD:128].astype(jnp.bfloat16)

    def partner(r, even, odd, late):
        zeros = jnp.zeros((ROWS, 256), jnp.float32)
        for n in range(PAIR):
            w = lax.bitwise_xor(mine, 2 * r + n)
            for m in range(MATCH):
                cut = [t_ref[c, m, w].astype(jnp.float32) for c in range(BLOCKS)]
                row = jnp.concatenate([zeros] + cut + [zeros], axis=1)
                now = pltpu.roll(row, WIDE - 128 - offs[m], 1)
                both = jnp.concatenate([now, pltpu.roll(now, WIDE - 1, 1)], axis=0)
                change = (both[:, :WIDE - 128] - both[:, 128:]).astype(jnp.bfloat16)
                both = both.astype(jnp.bfloat16)
                for k in range(FINE // 2):
                    rows = pl.ds(128 * m + 16 * k, 16)

                    def shifted(p, block):
                        one = p[:, 128 * block:128 * (block + 1)]
                        if k == 0:
                            return one
                        return pltpu.roll(jnp.where(lane >= 2 * k, one, p[:, 128 * (block + 1):128 * (block + 2)]), 128 - 2 * k, 1)

                    for i in range(NEAR):
                        first = 128 * (n * NEAR + i)
                        even[rows, first:first + 128] = shifted(change, 2 * i)
                        late[rows, first:first + 128] = shifted(both, 2 * i + 1)
                    for i in range(NEAR - 1):
                        first = 128 * (n * (NEAR - 1) + i)
                        odd[rows, first:first + 128] = shifted(change, 2 * i + 1)

    def product(y, v, even, odd, late, fresh):
        def blocks(pick):
            return jnp.concatenate(
                [
                    jnp.concatenate([ref[n, pl.ds(PAD - 2 * FINE * q + 128 * i, 128), :] for n in range(PAIR) for ref, i in pick], axis=0)
                    for q in range(GROUPS // 2)
                ],
                axis=1,
            )

        near = [(y, 2 * i) for i in range(NEAR)]
        far = [(y, 2 * i + 1) for i in range(NEAR - 1)]
        sums = [(v, 2 * i) for i in range(NEAR - 1)] + [(y, 2 * NEAR - 2)]
        for j, (lhs, pick) in enumerate(((even, near), (late, sums), (odd, far))):
            r = jnp.dot(lhs[...], blocks(pick), preferred_element_type=jnp.float32)
            for q in range(GROUPS // 2):
                part = r[:, 128 * q:128 * (q + 1)]
                acc[j, q] = part if fresh else acc[j, q] + part

    for y in (y0, y1):
        for n in range(PAIR):
            y[n, :PAD, :] = jnp.zeros((PAD, 128), jnp.bfloat16)
            y[n, PAD + LEN + FINE:, :] = jnp.zeros((SPAN - LEN - FINE, 128), jnp.bfloat16)
    rounds = WINS // PAIR
    buffers = ((y0, v0, e0, d0, t0), (y1, v1, e1, d1, t1))
    source(0, *buffers[0][:2])
    partner(0, *buffers[0][2:])
    for r in range(rounds):
        if r + 1 < rounds:
            source(r + 1, *buffers[(r + 1) % 2][:2])
            partner(r + 1, *buffers[(r + 1) % 2][2:])
        product(*buffers[r % 2], r == 0)

    for top, sign, j in ((0, 1, 0), (1, -1, 2)):
        lanes = pl.ds(128 * top, 128)
        for m in range(MATCH):
            for b in range(0, ROWS, 2):

                def lags(q, row):
                    rows = pl.ds(128 * m + row, FINE, stride=ROWS)
                    return (acc[1, q, rows, :] + sign * acc[j, q, rows, :]) * SCALE

                rows = []
                for q in range(GROUPS // 2):
                    lo, hi = lags(q, b), lags(q, b + 1)
                    rows.append(jnp.where(lane < CHANS, lo, pltpu.roll(hi, CHANS, 1)))
                    rows.append(jnp.where(lane < CHANS, pltpu.roll(lo, CHANS, 1), hi))
                z = jnp.concatenate(rows, axis=0).T
                o_ref[b, m, :, lanes] = z[:CHANS]
                o_ref[b + 1, m, :, lanes] = z[CHANS:]


def corr(offs, sources, partner):
    vmem = pl.BlockSpec(memory_space=pltpu.VMEM)
    return pl.pallas_call(
        corr_kernel,
        out_shape=jax.ShapeDtypeStruct((ROWS, MATCH, CHANS, LAGS), jnp.float32),
        in_specs=[pl.BlockSpec(memory_space=pltpu.SMEM)] + [vmem] * 5,
        out_specs=vmem,
        scratch_shapes=[pltpu.VMEM((PAIR, PAD + SPAN, 128), jnp.bfloat16)] * 2
        + [pltpu.VMEM((PAIR, PAD + LEN + FINE - 128, 128), jnp.bfloat16)] * 2
        + [pltpu.VMEM((MATCH * FINE * ROWS, PAIR * NEAR * 128), jnp.bfloat16)] * 2
        + [pltpu.VMEM((MATCH * FINE * ROWS, PAIR * (NEAR - 1) * 128), jnp.bfloat16)] * 2
        + [pltpu.VMEM((MATCH * FINE * ROWS, PAIR * NEAR * 128), jnp.bfloat16)] * 2
        + [pltpu.VMEM((3, GROUPS // 2, MATCH * FINE * ROWS, 128), jnp.float32)],
        compiler_params=pltpu.CompilerParams(vmem_limit_bytes=36 << 20),
        name="corr",
    )(offs, *sources, partner)


def local(waves, matchings, lag_offset):
    win = lax.axis_index("win")
    offs = lax.dynamic_index_in_dim(lag_offset, lax.axis_index("chan"), 1, keepdims=False)
    offs = jnp.concatenate([offs, jnp.full((1,), win, jnp.int32)])
    cut, turned = whiten(waves)
    chunks = lax.all_to_all(cut.reshape(BLOCKS * WINS, ROWS, 128), ("chan", "win"), 0, 0)
    other = lax.ppermute(turned, "win", [(i, i ^ 1) for i in range(WINS)])
    pair = jnp.stack([turned, other])
    far = []
    for r in (1, 2, 3):
        far.append(lax.ppermute(pair, "win", [(i, i ^ (2 * r)) for i in range(WINS)]))
    sent = choose(matchings, chunks.reshape(BLOCKS, WINS, ROWS, 128))
    partner = lax.all_to_all(sent, "chan", 0, 0)
    return corr(offs, [pair] + far, partner)


def solution(mesh):
    return jax.shard_map(
        local,
        mesh=mesh,
        in_specs=(P("chan", "win"), P(), P()),
        out_specs=P("win", None, "chan", None),
        check_vma=False,
    )
```

```python
import jax
import jax.numpy as jnp
from jax import lax
from jax.experimental import pallas as pl
from jax.experimental.pallas import tpu as pltpu
from jax.sharding import PartitionSpec as P

CHANS = 64
LEN = 2048
HALF = LEN // 2
BLOCKS = 16
WINS = 8
MATCH = 3
LAGS = 256
ROWS = CHANS // WINS
FINE = 16
GROUPS = 128 // FINE
SPAN = LEN + 128
WIDE = LEN + 512
PAD = 96
PAIR = 2
NEAR = (SPAN // 128 + 1) // 2
SCALE = 1.0 / 128.0


def whitened(x):
    power = jnp.mean(x * x, axis=1, keepdims=True)
    return x / jnp.sqrt(power + 1e-06)


def cut_kernel(x_ref, cut_ref):
    white = whitened(x_ref[...])
    for c in range(BLOCKS):
        for g in range(WINS):
            cut_ref[c, g] = white[g * ROWS:(g + 1) * ROWS, 128 * c:128 * (c + 1)].astype(jnp.bfloat16)


def turn_kernel(x_ref, turned_ref):
    white = whitened(x_ref[...])
    halves = jnp.concatenate([white[:, :HALF], white[:, HALF:]], axis=0)
    turned_ref[...] = halves.T.astype(jnp.bfloat16)


def whiten(kernel, shape, x):
    return pl.pallas_call(
        kernel,
        out_shape=jax.ShapeDtypeStruct(shape, jnp.bfloat16),
        compiler_params=pltpu.CompilerParams(vmem_limit_bytes=4 << 20),
        name="whiten",
    )(x)


def choose_kernel(match_ref, from_ref, to_ref):
    for d in range(BLOCKS):
        for m in range(MATCH):
            to_ref[d, m] = from_ref[match_ref[m, d]]


def choose(matchings, chunks):
    return pl.pallas_call(
        choose_kernel,
        out_shape=jax.ShapeDtypeStruct((BLOCKS, MATCH, WINS, ROWS, 128), jnp.bfloat16),
        in_specs=[pl.BlockSpec(memory_space=pltpu.SMEM), pl.BlockSpec(memory_space=pltpu.VMEM)],
        compiler_params=pltpu.CompilerParams(vmem_limit_bytes=4 << 20),
        name="choose",
    )(matchings, chunks)


def corr_kernel(offs, s0_ref, s1_ref, s2_ref, s3_ref, s4_ref, s5_ref, s6_ref, s7_ref, t_ref, o_ref, y0, y1, v0, v1, e0, e1, d0, d1, t0, t1, acc):
    lane = lax.broadcasted_iota(jnp.int32, (1, 128), 1)
    mine = offs[MATCH]
    sources = (s0_ref, s1_ref, s2_ref, s3_ref, s4_ref, s5_ref, s6_ref, s7_ref)

    def source(r, y, v):
        for n in range(PAIR):
            x = sources[PAIR * r + n][...].astype(jnp.float32)
            swapped = pltpu.roll(x, CHANS, 1)
            gap = jnp.zeros((FINE, 128), jnp.float32)
            now = jnp.concatenate([x, swapped, gap], axis=0)
            late = jnp.concatenate([gap, swapped, x], axis=0)
            both = jnp.where(lane < CHANS, now, late)
            y[n, PAD:PAD + LEN + FINE, :] = both.astype(jnp.bfloat16)
            v[n, PAD:PAD + LEN + FINE - 128, :] = (both[:-128] + both[128:]).astype(jnp.bfloat16)
            v[n, :PAD, :] = both[128 - PAD:128].astype(jnp.bfloat16)

    def partner(r, even, odd, late):
        zeros = jnp.zeros((ROWS, 256), jnp.float32)
        for n in range(PAIR):
            w = lax.bitwise_xor(mine, 2 * r + n)
            for m in range(MATCH):
                cut = [t_ref[c, m, w].astype(jnp.float32) for c in range(BLOCKS)]
                row = jnp.concatenate([zeros] + cut + [zeros], axis=1)
                now = pltpu.roll(row, WIDE - 128 - offs[m], 1)
                both = jnp.concatenate([now, pltpu.roll(now, WIDE - 1, 1)], axis=0)
                change = (both[:, :WIDE - 128] - both[:, 128:]).astype(jnp.bfloat16)
                both = both.astype(jnp.bfloat16)
                for k in range(FINE // 2):
                    rows = pl.ds(128 * m + 16 * k, 16)

                    def shifted(p, block):
                        one = p[:, 128 * block:128 * (block + 1)]
                        if k == 0:
                            return one
                        return pltpu.roll(jnp.where(lane >= 2 * k, one, p[:, 128 * (block + 1):128 * (block + 2)]), 128 - 2 * k, 1)

                    for i in range(NEAR):
                        first = 128 * (n * NEAR + i)
                        even[rows, first:first + 128] = shifted(change, 2 * i)
                        late[rows, first:first + 128] = shifted(both, 2 * i + 1)
                    for i in range(NEAR - 1):
                        first = 128 * (n * (NEAR - 1) + i)
                        odd[rows, first:first + 128] = shifted(change, 2 * i + 1)

    def product(y, v, even, odd, late, fresh):
        def blocks(pick):
            return jnp.concatenate(
                [
                    jnp.concatenate([ref[n, pl.ds(PAD - 2 * FINE * q + 128 * i, 128), :] for n in range(PAIR) for ref, i in pick], axis=0)
                    for q in range(GROUPS // 2)
                ],
                axis=1,
            )

        near = [(y, 2 * i) for i in range(NEAR)]
        far = [(y, 2 * i + 1) for i in range(NEAR - 1)]
        sums = [(v, 2 * i) for i in range(NEAR - 1)] + [(y, 2 * NEAR - 2)]
        for j, (lhs, pick) in enumerate(((even, near), (late, sums), (odd, far))):
            r = jnp.dot(lhs[...], blocks(pick), preferred_element_type=jnp.float32)
            for q in range(GROUPS // 2):
                part = r[:, 128 * q:128 * (q + 1)]
                acc[j, q] = part if fresh else acc[j, q] + part

    for y in (y0, y1):
        for n in range(PAIR):
            y[n, :PAD, :] = jnp.zeros((PAD, 128), jnp.bfloat16)
            y[n, PAD + LEN + FINE:, :] = jnp.zeros((SPAN - LEN - FINE, 128), jnp.bfloat16)
    rounds = WINS // PAIR
    buffers = ((y0, v0, e0, d0, t0), (y1, v1, e1, d1, t1))
    source(0, *buffers[0][:2])
    partner(0, *buffers[0][2:])
    for r in range(rounds):
        if r + 1 < rounds:
            source(r + 1, *buffers[(r + 1) % 2][:2])
            partner(r + 1, *buffers[(r + 1) % 2][2:])
        product(*buffers[r % 2], r == 0)

    for top, sign, j in ((0, 1, 0), (1, -1, 2)):
        lanes = pl.ds(128 * top, 128)
        for m in range(MATCH):
            for b in range(0, ROWS, 2):

                def lags(q, row):
                    rows = pl.ds(128 * m + row, FINE, stride=ROWS)
                    return (acc[1, q, rows, :] + sign * acc[j, q, rows, :]) * SCALE

                rows = []
                for q in range(GROUPS // 2):
                    lo, hi = lags(q, b), lags(q, b + 1)
                    rows.append(jnp.where(lane < CHANS, lo, pltpu.roll(hi, CHANS, 1)))
                    rows.append(jnp.where(lane < CHANS, pltpu.roll(lo, CHANS, 1), hi))
                z = jnp.concatenate(rows, axis=0).T
                o_ref[b, m, :, lanes] = z[:CHANS]
                o_ref[b + 1, m, :, lanes] = z[CHANS:]


def corr(offs, sources, partner):
    vmem = pl.BlockSpec(memory_space=pltpu.VMEM)
    return pl.pallas_call(
        corr_kernel,
        out_shape=jax.ShapeDtypeStruct((ROWS, MATCH, CHANS, LAGS), jnp.float32),
        in_specs=[pl.BlockSpec(memory_space=pltpu.SMEM)] + [vmem] * (WINS + 1),
        out_specs=vmem,
        scratch_shapes=[pltpu.VMEM((PAIR, PAD + SPAN, 128), jnp.bfloat16)] * 2
        + [pltpu.VMEM((PAIR, PAD + LEN + FINE - 128, 128), jnp.bfloat16)] * 2
        + [pltpu.VMEM((MATCH * FINE * ROWS, PAIR * NEAR * 128), jnp.bfloat16)] * 2
        + [pltpu.VMEM((MATCH * FINE * ROWS, PAIR * (NEAR - 1) * 128), jnp.bfloat16)] * 2
        + [pltpu.VMEM((MATCH * FINE * ROWS, PAIR * NEAR * 128), jnp.bfloat16)] * 2
        + [pltpu.VMEM((3, GROUPS // 2, MATCH * FINE * ROWS, 128), jnp.float32)],
        compiler_params=pltpu.CompilerParams(vmem_limit_bytes=36 << 20),
        name="corr",
    )(offs, *sources, partner)


def local(waves, matchings, lag_offset):
    win = lax.axis_index("win")
    offs = lax.dynamic_index_in_dim(lag_offset, lax.axis_index("chan"), 1, keepdims=False)
    offs = jnp.concatenate([offs, jnp.full((1,), win, jnp.int32)])
    cut = whiten(cut_kernel, (BLOCKS, WINS, ROWS, 128), waves)
    chunks = lax.all_to_all(cut.reshape(BLOCKS * WINS, ROWS, 128), ("chan", "win"), 0, 0)

    def sent_to(piece, flip):
        return lax.ppermute(piece, "win", [(i, i ^ flip) for i in range(WINS)])

    turned = whiten(turn_kernel, (HALF, 128), waves)
    other = sent_to(turned, 1)
    sources = [turned, other]
    for r in (1, 2, 3):
        sources.append(sent_to(turned, 2 * r))
        sources.append(sent_to(other, 2 * r))
    table = jnp.clip(matchings, 0, BLOCKS - 1)
    sent = choose(table, chunks.reshape(BLOCKS, WINS, ROWS, 128))
    partner = lax.all_to_all(sent, "chan", 0, 0)
    return corr(offs, sources, partner)


def solution(mesh):
    return jax.shard_map(
        local,
        mesh=mesh,
        in_specs=(P("chan", "win"), P(), P()),
        out_specs=P("win", None, "chan", None),
        check_vma=False,
    )
```
